32 devices in a mesh: fsdp: 16 (over z, y, core), tp: 2 (over x).
Axes of the slice: x: 2, y: 2, z: 4, core: 2. Of those that a mesh axis runs over, the one named last changes fastest.
Arguments:
- tokens_in: bfloat16 [4096, 2048], P(('fsdp', 'tp')), may hold values from -6 to 6
- cotangent: bfloat16 [4096, 2048], P(('fsdp', 'tp')), may hold values from -6 to 6
- w_query: bfloat16 [2048, 2048], P('fsdp', 'tp'), may hold values from -0.125 to 0.125
- w_key: bfloat16 [2048, 2048], P('fsdp', 'tp'), may hold values from -0.125 to 0.125
- w_value: bfloat16 [2048, 2048], P('fsdp', 'tp'), may hold values from -0.125 to 0.125
- w_output: bfloat16 [2048, 2048], P('tp', 'fsdp'), may hold values from -1 to 1
- gain_query: bfloat16 [16, 128], P('tp', 'fsdp'), may hold values from 0.25 to 1.75
- gain_key: bfloat16 [16, 128], P('tp', 'fsdp'), may hold values from 0.25 to 1.75
- gain_attn: bfloat16 [2048], P('fsdp'), may hold values from 0.25 to 1.75
- gain_moe: bfloat16 [2048], P('fsdp'), may hold values from 0.25 to 1.75
- w_router: bfloat16 [2048, 16], P('fsdp'), may hold values from -0.0625 to 0.0625
- w_gate: bfloat16 [16, 2048, 1024], P('fsdp', None, 'tp'), may hold values from -0.125 to 0.125
- w_up: bfloat16 [16, 2048, 1024], P('fsdp', None, 'tp'), may hold values from -0.125 to 0.125
- w_down: bfloat16 [16, 1024, 2048], P('fsdp', 'tp'), may hold values from -0.75 to 0.75
- expert_ids: int32 [4096, 8], P('fsdp'), may hold values from 0 to 15, all different within a row; in each aligned block of 256 rows (0 to 255, 256 to 511, ...) at most 152 rows name the same one
Outputs:
- block_out: float32 [4096, 2048], P(('fsdp', 'tp'))
- grad_tokens: float32 [4096, 2048], P(('fsdp', 'tp'))
- grad_query: float32 [2048, 2048], P('fsdp', 'tp')
- grad_key: float32 [2048, 2048], P('fsdp', 'tp')
- grad_value: float32 [2048, 2048], P('fsdp', 'tp')
- grad_output: float32 [2048, 2048], P('tp', 'fsdp')
- grad_gain_query: float32 [16, 128], P('tp', 'fsdp')
- grad_gain_key: float32 [16, 128], P('tp', 'fsdp')
- grad_gain_attn: float32 [2048], P('fsdp')
- grad_gain_moe: float32 [2048], P('fsdp')
- grad_router: float32 [2048, 16], P('fsdp')
- grad_gate: float32 [16, 2048, 1024], P('fsdp', None, 'tp')
- grad_up: float32 [16, 2048, 1024], P('fsdp', None, 'tp')
- grad_down: float32 [16, 1024, 2048], P('fsdp', 'tp')
The draws below stay inside these ranges and needn't reach their ends.
Inputs may be any that keep to these rules, and one draw needn't show every extreme that they name: `expert_ids`: each row names 8 different experts. In each aligned block of 256 rows (one group) no expert is named by more than 152 rows, a bound that some block reaches.
All inputs are finite; a program needn't handle non-finite values.
Results may differ from the reference program's by a relative error of at most 0.018.
Values may be sent and summed in bfloat16 or wider, within the bound.
No kernel may reach another device: no remote copies, remote signals or barrier semaphores. Data moves between devices by JAX's collectives and lax.ppermute only.
A program may use at most 256 MiB of HBM per device.

```python
import math
import jax
import jax.numpy as jnp
import numpy as np
from jax import lax

D = 2048
HEADS = 16
HEAD = 128
FF = 1024
TOPK = 8
PROMPT = 128
CONT_LEN = 64
EXPERTS = 16
GROUP = 256
TOKENS = 4096
CAP = 152
N_FSDP = 16
N_TP = 2


def spiked(drawn, rng, source, target, shards_of, factor):
    owner, partner = [(jnp.arange(drawn.shape[axis_at]) // (drawn.shape[axis_at] // shards_of)).reshape([-1 if axis == axis_at else 1 for axis in range(drawn.ndim)]) for axis_at in (source, target)]
    chosen = jax.random.permutation(rng, shards_of)[partner]
    strong = (owner == chosen) | (owner == (partner + shards_of // 2) % shards_of)
    return jnp.where(strong, factor * drawn, drawn)


def block_levels(rng, dims, cuts, low, top_value):
    level, own = 1.0, jax.random.fold_in(rng, 6)
    for axis_at, parts in cuts:
        heights = jnp.exp(jax.random.uniform(jax.random.fold_in(own, axis_at), (parts,), jnp.float32, low / len(cuts), top_value / len(cuts)))
        level = level * jnp.repeat(heights, dims[axis_at] // parts).reshape([-1 if axis == axis_at else 1 for axis in range(len(dims))])
    return level


def assign_block(key, own, number, rows, amount, top, limit, skew):
    ranking = jax.random.permutation(key, amount)
    packed, common = shares(amount, rows * top, limit, skew, True), shares(amount, rows * top, limit, skew, False)
    places = jnp.arange(amount)

    def named(tallies, rotation):
        used = int((tallies > 0).sum())
        fixed = max(1, used // 4)
        moved = fixed + (places - fixed + rotation * (used - fixed)) % max(1, amount - fixed)
        return jnp.zeros((amount,), jnp.int32).at[ranking[jnp.where(places < fixed, places, moved)]].set(jnp.asarray(tallies, jnp.int32))

    tallies = jnp.where(number % 4 == 0, named(packed, number // 4), named(common, number - number // 4 - 1))
    mixed = jax.random.permutation(jax.random.fold_in(own, 3), amount)
    source_of, receiver = mixed[0:amount // 2 * 2:2], mixed[1:amount // 2 * 2:2]
    slack = jnp.minimum(tallies[source_of] - 1, limit - tallies[receiver]) // 2
    slack = jnp.where((source_of == ranking[0]) | (receiver == ranking[0]) | (tallies[receiver] == 0), 0, jnp.maximum(slack, 0))
    moved = jax.random.randint(jax.random.fold_in(own, 4), (amount // 2,), 0, 1 << 20) % (slack + 1)
    tallies = tallies.at[source_of].add(-moved).at[receiver].add(moved)
    labels = jnp.searchsorted(jnp.cumsum(tallies), jnp.arange(rows * top), side="right").astype(jnp.int32)
    listing = labels.reshape(top, rows).T
    listing = listing[jax.random.permutation(jax.random.fold_in(own, 1), rows)]
    rotation = jax.random.randint(jax.random.fold_in(own, 2), (rows, 1), 0, top)
    return jnp.take_along_axis(listing, (jnp.arange(top)[None, :] + rotation) % top, axis=1)


def shares(number_of, total, most, skew, full):
    loads = [(1 << 20) // math.isqrt(grade ** skew) + 1 for grade in range(1, number_of + 1)]
    largest = most if full else min(most, max(-(-total // number_of), total * loads[0] // sum(loads)))
    least = 1 if total - largest >= number_of - 1 else 0
    holding, spare = [largest] + [least] * (number_of - 1), total - largest - least * (number_of - 1)
    while spare > 0:
        candidates = [i for i in range(1, number_of) if holding[i] < largest] or [i for i in range(1, number_of) if holding[i] < most]
        mass, remaining = sum([loads[i] for i in candidates]), spare
        for i in candidates:
            extra = min(most - holding[i], max(1, remaining * loads[i] // mass), spare)
            holding[i] = holding[i] + extra
            spare = spare - extra
    return np.array(holding)


def gaussian(rng, extent, deviation, limit, split=(), kind=jnp.bfloat16):
    level = block_levels(rng, extent, split, -0.22, 0.18) if split else 1.0
    entries = jax.random.normal(rng, extent, jnp.float32) * deviation * level
    return jnp.minimum(jnp.maximum(entries, -limit), limit).astype(kind)


def noise_with(stream_key, dims, spread, bound, split, heavy, held_as=jnp.bfloat16):
    values = spread * jax.random.normal(stream_key, dims, jnp.float32)
    if split:
        values = values * block_levels(stream_key, dims, split, -0.22, 0.18)
    return jnp.clip(spiked(values, jax.random.fold_in(stream_key, 3), *heavy), -bound, bound).astype(held_as)


def setup_inputs(seed: int = 0) -> dict:
    arg_keys = jax.random.split(jax.random.key(seed), 16)
    tokens_in = gaussian(arg_keys[0], (TOKENS, D), 1.0, 6.0, ((0, 32),))
    cotangent = noise_with(arg_keys[1], (TOKENS, D), 1.0, 6.0, ((0, 32),), (0, 1, 32, 2.75))
    w_query = gaussian(arg_keys[2], (D, D), D ** -0.5, 0.125, ((0, 16), (1, 2)))
    w_key = gaussian(arg_keys[3], (D, D), D ** -0.5, 0.125, ((0, 16), (1, 2)))
    w_value = gaussian(arg_keys[4], (D, D), D ** -0.5, 0.125, ((0, 16), (1, 2)))
    w_output = gaussian(arg_keys[5], (D, D), (D // 64) ** -0.5, 1.0, ((0, 2), (1, 16)))
    gain_query = jnp.clip(1.0 + 0.15 * jax.random.normal(arg_keys[6], (HEADS, HEAD), jnp.float32), 0.25, 1.75).astype(jnp.bfloat16)
    gain_key = jnp.clip(1.0 + 0.15 * jax.random.normal(arg_keys[7], (HEADS, HEAD), jnp.float32), 0.25, 1.75).astype(jnp.bfloat16)
    gain_attn = jnp.clip(1.0 + 0.15 * jax.random.normal(arg_keys[8], (D,), jnp.float32), 0.25, 1.75).astype(jnp.bfloat16)
    gain_moe = jnp.clip(1.0 + 0.15 * jax.random.normal(arg_keys[9], (D,), jnp.float32), 0.25, 1.75).astype(jnp.bfloat16)
    w_router = gaussian(arg_keys[10], (D, EXPERTS), (4 * D) ** -0.5, 0.0625, ((0, 16),))
    w_gate = gaussian(arg_keys[11], (EXPERTS, D, FF), D ** -0.5, 0.125, ((0, 16), (2, 2)))
    w_up = gaussian(arg_keys[12], (EXPERTS, D, FF), D ** -0.5, 0.125, ((0, 16), (2, 2)))
    w_down = gaussian(arg_keys[13], (EXPERTS, FF, D), (FF // 16) ** -0.5, 0.75, ((0, 16), (1, 2)))
    expert_ids_keys = jax.random.split(jax.random.fold_in(arg_keys[14], 1), TOKENS // GROUP)
    expert_ids_turns = jax.random.permutation(jax.random.fold_in(arg_keys[14], 3), TOKENS // GROUP)
    expert_ids = jax.vmap(lambda own, number: assign_block(jax.random.fold_in(arg_keys[14], 2), own, number, GROUP, EXPERTS, TOPK, CAP, 1))(expert_ids_keys, expert_ids_turns).reshape((TOKENS, TOPK))
    return {"tokens_in": tokens_in, "cotangent": cotangent, "w_query": w_query, "w_key": w_key, "w_value": w_value, "w_output": w_output, "gain_query": gain_query, "gain_key": gain_key, "gain_attn": gain_attn, "gain_moe": gain_moe, "w_router": w_router, "w_gate": w_gate, "w_up": w_up, "w_down": w_down, "expert_ids": expert_ids}


@jax.custom_vjp
def low(v):
    return lax.optimization_barrier(v.astype(jnp.bfloat16)).astype(jnp.float32)

@jax.custom_vjp
def low_back(v):
    return v

def low_keep(v):
    return (low(v), None)

def low_pass(kept, grad):
    return (grad,)

def back_keep(v):
    return (v, None)

def back_low(kept, grad):
    return (low(grad),)
low.defvjp(low_keep, low_pass)
low_back.defvjp(back_keep, back_low)
epsilon = 1e-05
theta_base = 10000.0
masked_score = -1e+30

def product(left, right):
    return jnp.dot(left, right, precision=lax.Precision.HIGHEST, preferred_element_type=jnp.float32)

def rms_scale(values):
    return lax.rsqrt(lax.optimization_barrier(jnp.mean(values * values, axis=-1, keepdims=True)) + epsilon)

def rotate_half(values):
    middle = values.shape[-1] // 2
    return jnp.concatenate([-values[..., middle:], values[..., :middle]], axis=-1)

def positions_of(group_len):
    row_index = jnp.arange(group_len, dtype=jnp.int32)
    return jnp.where(row_index < PROMPT, row_index, PROMPT + (row_index - PROMPT) % CONT_LEN)

def attend_mask(group_len):
    row_index = jnp.arange(group_len, dtype=jnp.int32)
    query_pos = row_index[:, None]
    key_pos = row_index[None, :]
    query_cont = (query_pos - PROMPT) // CONT_LEN
    key_cont = (key_pos - PROMPT) // CONT_LEN
    return (key_pos <= query_pos) & ((key_pos < PROMPT) | (query_cont == key_cont))

def rotary_tables(group_len):
    where_pos = positions_of(group_len).astype(jnp.float32)
    frequency = theta_base ** (-2.0 * jnp.arange(HEAD // 2, dtype=jnp.float32) / HEAD)
    angles = where_pos[:, None] * frequency[None, :]
    angles = jnp.concatenate([angles, angles], axis=1)
    return (jnp.cos(angles), jnp.sin(angles))

def slot_table(routed):
    onehot = (routed[:, :, None] == jnp.arange(EXPERTS, dtype=jnp.int32)[None, None, :]).astype(jnp.int32)
    per_token = lax.optimization_barrier(jnp.sum(onehot, axis=1)).astype(jnp.int32)
    before = (jnp.cumsum(per_token, axis=0) - per_token).astype(jnp.int32)
    slot_index = lax.optimization_barrier(jnp.sum(onehot * before[:, None, :], axis=2)).astype(jnp.int32)
    return (routed * CAP + slot_index).astype(jnp.int32)

def group_layer(params, tokens, routed):
    w_query, w_key, w_value, w_output, gain_query, gain_key, gain_attn, gain_moe, w_router, w_gate, w_up, w_down = params
    group_len = tokens.shape[0]
    normed_one = low(tokens * rms_scale(tokens) * gain_attn)
    query_raw = low_back(product(normed_one, w_query))
    key_raw = low_back(product(normed_one, w_key))
    value_rows = low_back(low(product(normed_one, w_value)))
    query_norm = query_raw * rms_scale(query_raw) * gain_query.reshape(-1)
    key_norm = key_raw * rms_scale(key_raw) * gain_key.reshape(-1)
    cosine_table, sine_table = rotary_tables(group_len)

    def rotate(matrix):
        pieces = matrix.reshape(group_len, HEADS, HEAD)
        return pieces * cosine_table[:, None, :] + rotate_half(pieces) * sine_table[:, None, :]
    query_rot = low_back(low(rotate(query_norm)))
    key_rot = low_back(low(rotate(key_norm)))
    value_heads = value_rows.reshape(group_len, HEADS, HEAD)
    raw_scores = jnp.einsum('qhd,khd->hqk', query_rot, key_rot, precision=lax.Precision.HIGHEST) * HEAD ** (-0.5)
    scores = low_back(jnp.where(attend_mask(group_len)[None], raw_scores, masked_score))
    attn_probs = jax.nn.softmax(scores, axis=-1)
    context = jnp.einsum('hqk,khd->qhd', low(attn_probs), value_heads, precision=lax.Precision.HIGHEST)
    context = low_back(low(context.reshape(group_len, D)))
    hidden = tokens + low_back(product(context, w_output))
    normed_two = low(hidden * rms_scale(hidden) * gain_moe)
    logits = low_back(product(normed_two, w_router))
    gate_probs = jax.nn.softmax(jnp.take_along_axis(logits, routed, axis=1), axis=-1)
    slot_dest = slot_table(routed).reshape(-1)
    dispatch = jnp.zeros((EXPERTS * CAP, D), jnp.float32).at[slot_dest].set(jnp.repeat(normed_two, TOPK, axis=0))
    dispatch = dispatch.reshape(EXPERTS, CAP, D)
    part_width = FF // N_TP
    stacked = jnp.stack([low_back(dispatch) for part_index in range(N_TP)])
    gate_split = w_gate.reshape(EXPERTS, D, N_TP, part_width)
    up_split = w_up.reshape(EXPERTS, D, N_TP, part_width)
    down_split = w_down.reshape(EXPERTS, N_TP, part_width, D)
    gate_pre = low_back(jnp.einsum('pecd,edpf->pecf', stacked, gate_split, precision=lax.Precision.HIGHEST))
    up_pre = low_back(jnp.einsum('pecd,edpf->pecf', stacked, up_split, precision=lax.Precision.HIGHEST))
    activation = low(jax.nn.silu(gate_pre) * up_pre)
    partial_value = low_back(low(jnp.einsum('pecf,epfd->pecd', activation, down_split, precision=lax.Precision.HIGHEST)))
    expert_rows = lax.optimization_barrier(jnp.sum(partial_value, axis=0)).reshape(EXPERTS * CAP, D)
    gathered = expert_rows[slot_dest].reshape(group_len, TOPK, D)
    return hidden + lax.optimization_barrier(jnp.sum(gate_probs[:, :, None] * gathered, axis=1))

def reference(tokens_in, cotangent, w_query, w_key, w_value, w_output, gain_query, gain_key, gain_attn, gain_moe, w_router, w_gate, w_up, w_down, expert_ids):
    params = tuple((weight.astype(jnp.float32) for weight in (w_query, w_key, w_value, w_output, gain_query, gain_key, gain_attn, gain_moe, w_router, w_gate, w_up, w_down)))
    tokens = tokens_in.astype(jnp.float32).reshape(N_FSDP, GROUP, D)
    routed = expert_ids.astype(jnp.int32).reshape(N_FSDP, GROUP, TOPK)

    def forward(params_now, tokens_now):

        def one_group(group_pair):
            return group_layer(params_now, group_pair[0], group_pair[1])
        return lax.map(jax.checkpoint(one_group), (tokens_now, routed))
    outputs, pullback = jax.vjp(forward, params, tokens)
    grad_params, grad_rows = pullback(cotangent.astype(jnp.float32).reshape(N_FSDP, GROUP, D))
    grad_query, grad_key, grad_value, grad_output, grad_gain_query, grad_gain_key, grad_gain_attn, grad_gain_moe, grad_router, grad_gate, grad_up, grad_down = grad_params
    return (outputs.reshape(TOKENS, D), grad_rows.reshape(TOKENS, D), grad_query, grad_key, grad_value, grad_output, grad_gain_query, grad_gain_key, grad_gain_attn, grad_gain_moe, grad_router, grad_gate, grad_up, grad_down)
```

```python
import jax
import jax.numpy as jnp
from jax import lax
from jax.sharding import PartitionSpec as P

HEAD = 128
PROMPT = 128
CONT_LEN = 64


epsilon = 1e-05
theta_base = 10000.0
masked_score = -1e30


def rms_scale(values):
    return lax.rsqrt(jnp.mean(values * values, axis=-1, keepdims=True) + epsilon)


def rotate_half(values):
    middle = values.shape[-1] // 2
    return jnp.concatenate([-values[..., middle:], values[..., :middle]], axis=-1)


def rotate_back(values):
    middle = values.shape[-1] // 2
    return jnp.concatenate([values[..., middle:], -values[..., :middle]], axis=-1)


def positions_of(group_len):
    row_index = jnp.arange(group_len, dtype=jnp.int32)
    return jnp.where(row_index < PROMPT, row_index, PROMPT + (row_index - PROMPT) % CONT_LEN)


def attend_mask(group_len):
    row_index = jnp.arange(group_len, dtype=jnp.int32)
    query_pos = row_index[:, None]
    key_pos = row_index[None, :]
    query_cont = (query_pos - PROMPT) // CONT_LEN
    key_cont = (key_pos - PROMPT) // CONT_LEN
    return (key_pos <= query_pos) & ((key_pos < PROMPT) | (query_cont == key_cont))


def rotary_tables(group_len):
    where_pos = positions_of(group_len).astype(jnp.float32)
    frequency = theta_base ** (-2.0 * jnp.arange(HEAD // 2, dtype=jnp.float32) / HEAD)
    angles = where_pos[:, None] * frequency[None, :]
    angles = jnp.concatenate([angles, angles], axis=1)
    return (jnp.cos(angles), jnp.sin(angles))


def rounded(values):
    return lax.optimization_barrier(values.astype(jnp.bfloat16)).astype(jnp.float32)


def head_sums(first, second):
    return lax.psum((first, second), "tp")


def send_slots(block):
    return lax.all_to_all(block, "fsdp", split_axis=0, concat_axis=0, tiled=True)


def return_slots(block):
    return lax.all_to_all(block, "fsdp", split_axis=0, concat_axis=0, tiled=True)


def sparse_body(
    tokens_in,
    cotangent,
    w_query,
    w_key,
    w_value,
    w_output,
    gain_query,
    gain_key,
    gain_attn,
    gain_moe,
    w_router,
    w_gate,
    w_up,
    w_down,
    expert_ids,
):
    fsdp_count = lax.axis_size("fsdp")
    part_index = lax.axis_index("tp")
    own_rows = tokens_in.shape[0]
    start_row = part_index * own_rows

    def gather_params():
        return (
            lax.all_gather(w_query, "fsdp", axis=0, tiled=True),
            lax.all_gather(w_key, "fsdp", axis=0, tiled=True),
            lax.all_gather(w_value, "fsdp", axis=0, tiled=True),
            lax.all_gather(w_output, "fsdp", axis=1, tiled=True),
            lax.all_gather(gain_query, "fsdp", axis=1, tiled=True),
            lax.all_gather(gain_key, "fsdp", axis=1, tiled=True),
            lax.all_gather(gain_attn, "fsdp", axis=0, tiled=True),
            lax.all_gather(gain_moe, "fsdp", axis=0, tiled=True),
            lax.all_gather(w_router, "fsdp", axis=0, tiled=True),
        )

    (
        query_mat,
        key_mat,
        value_mat,
        output_mat,
        query_gain,
        key_gain,
        attn_gain,
        moe_gain,
        router_mat,
    ) = gather_params()
    rows_all, grad_rows = (
        lax.all_gather(tokens_in, "tp", axis=0, tiled=True),
        lax.all_gather(cotangent, "tp", axis=0, tiled=True),
    )
    group_len = rows_all.shape[0]
    model_width = rows_all.shape[1]
    topk_count = expert_ids.shape[1]
    expert_count = router_mat.shape[1]
    local_experts = w_gate.shape[0]
    capacity = (group_len * topk_count * 7 // (6 * expert_count) + 7) // 8 * 8
    slot_count = expert_count * capacity
    residual_in = rows_all.astype(jnp.float32)
    scale_one = rms_scale(residual_in)
    normal_one = residual_in * scale_one
    normed_one = (normal_one * attn_gain.astype(jnp.float32)).astype(jnp.bfloat16)
    query_raw = jnp.dot(normed_one, query_mat, preferred_element_type=jnp.float32)
    key_raw = jnp.dot(normed_one, key_mat, preferred_element_type=jnp.float32)
    value_flat = jnp.dot(normed_one, value_mat, preferred_element_type=jnp.float32).astype(
        jnp.bfloat16
    )
    query_sq, key_sq = head_sums(
        jnp.sum(query_raw * query_raw, axis=1), jnp.sum(key_raw * key_raw, axis=1)
    )
    query_scale = lax.rsqrt(query_sq / model_width + epsilon)[:, None]
    key_scale = lax.rsqrt(key_sq / model_width + epsilon)[:, None]
    heads_local = query_gain.shape[0]
    query_gain_flat = query_gain.astype(jnp.float32).reshape(-1)
    key_gain_flat = key_gain.astype(jnp.float32).reshape(-1)
    query_unit = query_raw * query_scale
    key_unit = key_raw * key_scale
    cosine_table, sine_table = rotary_tables(group_len)

    def rotate(matrix):
        pieces = matrix.reshape(group_len, heads_local, HEAD)
        return pieces * cosine_table[:, None, :] + rotate_half(pieces) * sine_table[:, None, :]

    query_rot = rotate(query_unit * query_gain_flat).astype(jnp.bfloat16)
    key_rot = rotate(key_unit * key_gain_flat).astype(jnp.bfloat16)
    value_heads = value_flat.reshape(group_len, heads_local, HEAD)
    allowed = attend_mask(group_len)[None]
    score_scale = HEAD ** (-0.5)

    def scores_now():
        raw_scores = (
            jnp.einsum("qhd,khd->hqk", query_rot, key_rot, preferred_element_type=jnp.float32)
            * score_scale
        )
        return jnp.where(allowed, raw_scores, masked_score)

    scores = scores_now()
    row_top = jnp.max(scores, axis=-1, keepdims=True)
    exp_scores = jnp.exp(scores - row_top)
    exp_total = jnp.sum(exp_scores, axis=-1, keepdims=True)
    log_total = row_top + jnp.log(exp_total)
    context = jnp.einsum(
        "hqk,khd->qhd",
        (exp_scores / exp_total).astype(jnp.bfloat16),
        value_heads,
        preferred_element_type=jnp.float32,
    )
    context_flat = context.reshape(group_len, -1).astype(jnp.bfloat16)
    attn_out = lax.psum(jnp.dot(context_flat, output_mat, preferred_element_type=jnp.float32), "tp")
    hidden = residual_in + attn_out
    scale_two = rms_scale(hidden)
    normal_two = hidden * scale_two
    normed_two = (normal_two * moe_gain.astype(jnp.float32)).astype(jnp.bfloat16)
    logits = jnp.dot(normed_two, router_mat, preferred_element_type=jnp.float32)
    onehot = expert_ids[:, :, None] == jnp.arange(expert_count, dtype=jnp.int32)[None, None, :]
    chosen = jnp.sum(jnp.where(onehot, logits[:, None, :], 0.0), axis=2)
    gate_probs = jax.nn.softmax(chosen, axis=-1)
    per_token = jnp.sum(onehot.astype(jnp.float32), axis=1)
    row_index = jnp.arange(group_len, dtype=jnp.int32)
    earlier = (row_index[None, :] < row_index[:, None]).astype(jnp.float32)
    before = jnp.dot(earlier, per_token, preferred_element_type=jnp.float32)
    slot_index = jnp.sum(jnp.where(onehot, before[:, None, :], 0.0), axis=2).astype(jnp.int32)
    slot_dest = expert_ids * capacity + slot_index
    flat_dest = slot_dest.reshape(-1)
    token_of_slot = (
        jnp.full((slot_count,), group_len, jnp.int32)
        .at[flat_dest]
        .set(jnp.repeat(row_index, topk_count))
    )
    gate_of_slot = jnp.zeros((slot_count,), jnp.float32).at[flat_dest].set(gate_probs.reshape(-1))
    slot_mine = slot_index >= 0
    normed_pad = jnp.concatenate([normed_two, jnp.zeros((1, model_width), jnp.bfloat16)], axis=0)
    cotangent_pad = jnp.concatenate([grad_rows, jnp.zeros((1, model_width), jnp.bfloat16)], axis=0)
    send_shape = (fsdp_count, local_experts, capacity, model_width)
    outgoing = normed_pad[token_of_slot].reshape(send_shape)
    arrived = send_slots(outgoing)
    gate_pre = jnp.einsum("secd,edf->secf", arrived, w_gate, preferred_element_type=jnp.float32)
    up_pre = jnp.einsum("secd,edf->secf", arrived, w_up, preferred_element_type=jnp.float32)
    gate_pre, up_pre, activation = (
        gate_pre,
        up_pre,
        (jax.nn.silu(gate_pre) * up_pre).astype(jnp.bfloat16),
    )
    partial_value = jnp.einsum(
        "secf,efd->secd", activation, w_down, preferred_element_type=jnp.float32
    ).astype(jnp.bfloat16)
    returned = return_slots(partial_value).reshape(-1, model_width)
    cotangent_full = grad_rows.astype(jnp.float32)
    moe_part = jnp.zeros((group_len, model_width), jnp.float32)
    gate_terms = []
    for column in range(topk_count):
        picked = jnp.where(
            slot_mine[:, column : column + 1],
            returned[slot_dest[:, column]].astype(jnp.float32),
            0.0,
        )
        moe_part = moe_part + gate_probs[:, column : column + 1] * picked
        gate_terms.append(jnp.sum(cotangent_full * picked, axis=1))
    moe_own = lax.psum_scatter(
        moe_part.astype(jnp.bfloat16), "tp", scatter_dimension=0, tiled=True
    ).astype(jnp.float32)
    block_out = lax.dynamic_slice_in_dim(hidden, start_row, own_rows, 0) + moe_own
    (
        query_mat,
        key_mat,
        value_mat,
        output_mat,
        query_gain,
        key_gain,
        attn_gain,
        moe_gain,
        router_mat,
    ) = gather_params()
    grad_slot = (
        (cotangent_pad[token_of_slot].astype(jnp.float32) * gate_of_slot[:, None])
        .astype(jnp.bfloat16)
        .reshape(send_shape)
    )
    grad_partial = send_slots(grad_slot)
    grad_act = jnp.einsum(
        "secd,efd->secf", grad_partial, w_down, preferred_element_type=jnp.float32
    )
    grad_down = jnp.einsum(
        "secf,secd->efd", activation, grad_partial, preferred_element_type=jnp.float32
    )
    gate_sig = jax.nn.sigmoid(gate_pre)
    grad_gate_pre = (grad_act * up_pre * gate_sig * (1.0 + gate_pre * (1.0 - gate_sig))).astype(
        jnp.bfloat16
    )
    grad_up_pre = (grad_act * gate_pre * gate_sig).astype(jnp.bfloat16)
    grad_gate = jnp.einsum(
        "secd,secf->edf", arrived, grad_gate_pre, preferred_element_type=jnp.float32
    )
    grad_up = jnp.einsum("secd,secf->edf", arrived, grad_up_pre, preferred_element_type=jnp.float32)
    grad_in = (
        jnp.einsum("secf,edf->secd", grad_gate_pre, w_gate, preferred_element_type=jnp.float32)
        + jnp.einsum("secf,edf->secd", grad_up_pre, w_up, preferred_element_type=jnp.float32)
    ).astype(jnp.bfloat16)
    grad_back = return_slots(grad_in).reshape(-1, model_width)
    grad_normed_part = jnp.zeros((group_len, model_width), jnp.float32)
    for column in range(topk_count):
        grad_normed_part = grad_normed_part + jnp.where(
            slot_mine[:, column : column + 1],
            grad_back[slot_dest[:, column]].astype(jnp.float32),
            0.0,
        )
    grad_normed_moe, grad_gate_probs = lax.psum(
        (grad_normed_part, jnp.stack(gate_terms, axis=1)), "tp"
    )
    grad_chosen = gate_probs * (
        grad_gate_probs - jnp.sum(gate_probs * grad_gate_probs, axis=1, keepdims=True)
    )
    grad_logits = jnp.sum(jnp.where(onehot, grad_chosen[:, :, None], 0.0), axis=1).astype(
        jnp.bfloat16
    )
    grad_router = jnp.einsum(
        "td,te->de", normed_two, grad_logits, preferred_element_type=jnp.float32
    )
    grad_normed_two = grad_normed_moe + jnp.einsum(
        "te,de->td", grad_logits, router_mat, preferred_element_type=jnp.float32
    )
    grad_gain_moe = jnp.sum(grad_normed_two * normal_two, axis=0)
    grad_unit_two = grad_normed_two * moe_gain.astype(jnp.float32)
    grad_hidden = cotangent_full + scale_two * (
        grad_unit_two - normal_two * jnp.mean(grad_unit_two * normal_two, axis=1, keepdims=True)
    )
    grad_attn = grad_hidden.astype(jnp.bfloat16)
    grad_output = jnp.einsum(
        "tc,td->cd", context_flat, grad_attn, preferred_element_type=jnp.float32
    )
    grad_context = (
        jnp.einsum("td,cd->tc", grad_attn, output_mat, preferred_element_type=jnp.float32)
        .astype(jnp.bfloat16)
        .reshape(group_len, heads_local, HEAD)
    )
    attn_probs = jnp.exp(scores_now() - log_total)
    grad_value_rows = (
        jnp.einsum(
            "hqk,qhd->khd",
            attn_probs.astype(jnp.bfloat16),
            grad_context,
            preferred_element_type=jnp.float32,
        )
        .reshape(group_len, -1)
        .astype(jnp.bfloat16)
    )
    grad_probs = jnp.einsum(
        "qhd,khd->hqk", grad_context, value_heads, preferred_element_type=jnp.float32
    )
    grad_scores = (
        attn_probs * (grad_probs - jnp.sum(attn_probs * grad_probs, axis=-1, keepdims=True))
    ).astype(jnp.bfloat16)
    grad_query_rot = rounded(
        jnp.einsum("hqk,khd->qhd", grad_scores, key_rot, preferred_element_type=jnp.float32)
        * score_scale
    )
    grad_key_rot = rounded(
        jnp.einsum("hqk,qhd->khd", grad_scores, query_rot, preferred_element_type=jnp.float32)
        * score_scale
    )

    def unrotate(grad_heads):
        return (
            grad_heads * cosine_table[:, None, :] + rotate_back(grad_heads * sine_table[:, None, :])
        ).reshape(group_len, -1)

    grad_query_norm = unrotate(grad_query_rot)
    grad_key_norm = unrotate(grad_key_rot)
    sum_query, sum_key = head_sums(
        jnp.sum(grad_query_norm * query_gain_flat * query_unit, axis=1),
        jnp.sum(grad_key_norm * key_gain_flat * key_unit, axis=1),
    )
    grad_query_raw = (
        query_scale
        * (query_gain_flat * grad_query_norm - query_unit * (sum_query / model_width)[:, None])
    ).astype(jnp.bfloat16)
    grad_key_raw = (
        key_scale * (key_gain_flat * grad_key_norm - key_unit * (sum_key / model_width)[:, None])
    ).astype(jnp.bfloat16)
    grad_gain_query = jnp.sum(grad_query_norm * query_unit, axis=0).reshape(heads_local, HEAD)
    grad_gain_key = jnp.sum(grad_key_norm * key_unit, axis=0).reshape(heads_local, HEAD)
    grad_query = jnp.einsum(
        "td,tc->dc", normed_one, grad_query_raw, preferred_element_type=jnp.float32
    )
    grad_key = jnp.einsum("td,tc->dc", normed_one, grad_key_raw, preferred_element_type=jnp.float32)
    grad_value = jnp.einsum(
        "td,tc->dc", normed_one, grad_value_rows, preferred_element_type=jnp.float32
    )
    grad_normed_local = (
        jnp.einsum("tc,dc->td", grad_query_raw, query_mat, preferred_element_type=jnp.float32)
        + jnp.einsum("tc,dc->td", grad_key_raw, key_mat, preferred_element_type=jnp.float32)
        + jnp.einsum("tc,dc->td", grad_value_rows, value_mat, preferred_element_type=jnp.float32)
    )
    grad_normed_one = lax.psum(grad_normed_local.astype(jnp.bfloat16), "tp").astype(jnp.float32)
    grad_gain_attn = jnp.sum(grad_normed_one * normal_one, axis=0)
    grad_unit_one = grad_normed_one * attn_gain.astype(jnp.float32)
    grad_full = grad_hidden + scale_one * (
        grad_unit_one - normal_one * jnp.mean(grad_unit_one * normal_one, axis=1, keepdims=True)
    )
    grad_tokens = lax.dynamic_slice_in_dim(grad_full, start_row, own_rows, 0)
    sharded = (
        lax.psum_scatter(grad_query, "fsdp", scatter_dimension=0, tiled=True),
        lax.psum_scatter(grad_key, "fsdp", scatter_dimension=0, tiled=True),
        lax.psum_scatter(grad_value, "fsdp", scatter_dimension=0, tiled=True),
        lax.psum_scatter(grad_output, "fsdp", scatter_dimension=1, tiled=True),
        lax.psum_scatter(grad_gain_query, "fsdp", scatter_dimension=1, tiled=True),
        lax.psum_scatter(grad_gain_key, "fsdp", scatter_dimension=1, tiled=True),
        lax.psum_scatter(grad_gain_attn, "fsdp", scatter_dimension=0, tiled=True),
        lax.psum_scatter(grad_gain_moe, "fsdp", scatter_dimension=0, tiled=True),
        lax.psum_scatter(grad_router, "fsdp", scatter_dimension=0, tiled=True),
    )
    return (
        block_out,
        grad_tokens,
        sharded[0],
        sharded[1],
        sharded[2],
        sharded[3],
        sharded[4],
        sharded[5],
        sharded[6],
        sharded[7],
        sharded[8],
        grad_gate,
        grad_up,
        grad_down,
    )


def swap_tp(values):
    return lax.ppermute(values, "tp", [(0, 1), (1, 0)])


def joined_rows(own, other, part_index):
    first = jnp.where(part_index == 0, own, other)
    second = jnp.where(part_index == 0, other, own)
    return jnp.concatenate([first, second], axis=0)


def halves_of(values, part_index):
    rows = values.shape[0] // 2
    low, high = values[:rows], values[rows:]
    return jnp.where(part_index == 0, low, high), jnp.where(part_index == 0, high, low)


def dense_body(
    tokens_in,
    cotangent,
    w_query,
    w_key,
    w_value,
    w_output,
    gain_query,
    gain_key,
    gain_attn,
    gain_moe,
    w_router,
    w_gate,
    w_up,
    w_down,
    expert_ids,
):
    f32, bf16 = jnp.float32, jnp.bfloat16
    fsdp_count = lax.axis_size("fsdp")
    part_index = lax.axis_index("tp")
    expert_index = lax.axis_index("fsdp")
    own_rows, model_width = tokens_in.shape
    group_len = 2 * own_rows
    half_width = w_query.shape[1]
    topk_count = expert_ids.shape[1]
    expert_count = w_router.shape[1]
    shard_rows = w_query.shape[0]
    heads_local = gain_query.shape[0]
    gain_cols = gain_query.shape[1]
    capacity = (group_len * topk_count * 7 // (6 * expert_count) + 7) // 8 * 8

    def dot(left, right, dims):
        return lax.dot_general(left, right, (dims, ((), ())), preferred_element_type=f32)

    def column(flat):
        return jnp.pad(flat, (0, shard_rows - flat.shape[0]))[:, None]

    small = jnp.concatenate(
        [
            w_router,
            gain_attn[:, None],
            gain_moe[:, None],
            column(gain_query.reshape(-1)),
            column(gain_key.reshape(-1)),
        ],
        axis=1,
    )
    small_cols = small.shape[1]
    small = jnp.pad(small, ((0, 0), (0, 128 - small_cols)))
    packed = jnp.concatenate([w_query, w_key, w_value, small], axis=1)
    packed_all = lax.all_gather(packed, "fsdp", axis=0, tiled=True)
    qkv_mat = packed_all[:, : 3 * half_width]
    small_all = packed_all[:, 3 * half_width :]
    router_mat = small_all[:, :expert_count]
    attn_gain = small_all[:, expert_count].astype(f32)
    moe_gain = small_all[:, expert_count + 1].astype(f32)

    def head_gain(index):
        flat = small_all[:, expert_count + 2 + index].reshape(fsdp_count, shard_rows)
        flat = flat[:, : heads_local * gain_cols].reshape(fsdp_count, heads_local, gain_cols)
        return jnp.transpose(flat, (1, 0, 2)).reshape(-1).astype(f32)

    query_gain_flat, key_gain_flat = head_gain(0), head_gain(1)
    out_mat_t = lax.all_gather(w_output.T, "fsdp", axis=0, tiled=True)
    ids_all = lax.all_gather(expert_ids, "fsdp", axis=0, tiled=True)

    residual_in = joined_rows(tokens_in, swap_tp(tokens_in), part_index).astype(f32)
    scale_one = rms_scale(residual_in)
    normed_one = (residual_in * scale_one * attn_gain).astype(bf16)
    qkv = dot(normed_one, qkv_mat, ((1,), (0,)))
    query_raw = qkv[:, :half_width]
    key_raw = qkv[:, half_width : 2 * half_width]
    value_flat = qkv[:, 2 * half_width :].astype(bf16)
    squares = jnp.stack(
        [jnp.sum(query_raw * query_raw, axis=1), jnp.sum(key_raw * key_raw, axis=1)]
    )
    squares = squares + swap_tp(squares)
    query_scale = lax.rsqrt(squares[0] / model_width + epsilon)[:, None]
    key_scale = lax.rsqrt(squares[1] / model_width + epsilon)[:, None]
    query_unit = query_raw * query_scale
    key_unit = key_raw * key_scale
    cosine_table, sine_table = rotary_tables(group_len)

    def rotate(matrix):
        pieces = matrix.reshape(group_len, heads_local, HEAD)
        return pieces * cosine_table[:, None, :] + rotate_half(pieces) * sine_table[:, None, :]

    query_rot = rotate(query_unit * query_gain_flat).astype(bf16)
    key_rot = rotate(key_unit * key_gain_flat).astype(bf16)
    value_heads = value_flat.reshape(group_len, heads_local, HEAD)
    allowed = attend_mask(group_len)[None]
    score_scale = HEAD ** (-0.5)
    raw_scores = (
        jnp.einsum("qhd,khd->hqk", query_rot, key_rot, preferred_element_type=f32) * score_scale
    )
    scores = jnp.where(allowed, raw_scores, masked_score)
    row_top = jnp.max(scores, axis=-1, keepdims=True)
    exp_scores = jnp.exp(scores - row_top)
    attn_probs = exp_scores / jnp.sum(exp_scores, axis=-1, keepdims=True)
    probs_low = attn_probs.astype(bf16)
    context = jnp.einsum("hqk,khd->qhd", probs_low, value_heads, preferred_element_type=f32)
    context_flat = context.reshape(group_len, -1).astype(bf16)
    attn_part = dot(context_flat, out_mat_t, ((1,), (1,)))
    attn_own, attn_other = halves_of(attn_part, part_index)
    tokens_own = tokens_in.astype(f32)
    hidden = tokens_own + (attn_own + swap_tp(attn_other.astype(bf16)).astype(f32))
    scale_two = rms_scale(hidden)
    normal_two = hidden * scale_two
    normed_two = (normal_two * moe_gain).astype(bf16)

    both = ("fsdp", "tp")
    rows_all = lax.all_gather(normed_two, both, axis=0, tiled=True)
    cotangent_all = lax.all_gather(cotangent, both, axis=0, tiled=True)
    expert_row = jnp.arange(expert_count, dtype=jnp.int32)

    def chosen_mask(ids):
        return jnp.any(ids[:, :, None] == expert_row[None, None, :], axis=1)

    def gates_of(rows, mask):
        logits = jnp.where(mask, dot(rows, router_mat, ((1,), (0,))), -jnp.inf)
        top = jnp.max(logits, axis=1, keepdims=True)
        weights = jnp.where(mask, jnp.exp(logits - top), 0.0)
        return weights / jnp.sum(weights, axis=1, keepdims=True)

    gates_all = gates_of(rows_all, chosen_mask(ids_all))
    gate_here = jnp.sum(jnp.where(expert_row[None, :] == expert_index, gates_all, 0.0), axis=1)
    gate_here = gate_here.reshape(fsdp_count, group_len)
    named = jnp.any(ids_all == expert_index, axis=1).reshape(fsdp_count, group_len)
    row_index = jnp.arange(group_len, dtype=jnp.int32)
    earlier = (row_index[:, None] < row_index[None, :]).astype(bf16)
    place = dot(named.astype(bf16), earlier, ((1,), (0,))).astype(jnp.int32)
    slot_row = jnp.arange(capacity, dtype=jnp.int32)
    select = (slot_row[None, :, None] == place[:, None, :]) & named[:, None, :]
    select_low = select.astype(bf16)
    gate_slot = jnp.sum(jnp.where(select, gate_here[:, None, :], 0.0), axis=2)

    def pick(rows):
        grouped = rows.reshape(fsdp_count, group_len, model_width)
        return jnp.einsum("gct,gtd->gcd", select_low, grouped, preferred_element_type=f32)

    def spread(slots):
        return jnp.einsum("gct,gcd->gtd", select_low, slots, preferred_element_type=f32)

    slot_count = fsdp_count * capacity
    arrived = pick(rows_all).astype(bf16).reshape(slot_count, model_width)
    gate_mat, up_mat, down_mat = w_gate[0], w_up[0], w_down[0]
    gate_pre = dot(arrived, gate_mat, ((1,), (0,)))
    up_pre = dot(arrived, up_mat, ((1,), (0,)))
    gate_sig = jax.nn.sigmoid(gate_pre)
    activation = (gate_pre * gate_sig * up_pre).astype(bf16)
    partial_value = dot(activation, down_mat, ((1,), (0,))).astype(bf16)
    partial_value = partial_value.reshape(fsdp_count, capacity, model_width)
    cotangent_slot = pick(cotangent_all)
    slot_dots = jnp.sum(cotangent_slot * partial_value.astype(f32), axis=2)
    token_dots = jnp.sum(jnp.where(select, slot_dots[:, :, None], 0.0), axis=1)
    moe_out = (spread(partial_value) * gate_here[:, :, None]).astype(bf16)
    moe_out = moe_out.reshape(-1, model_width)
    dots_owned = lax.all_to_all(token_dots, "fsdp", split_axis=0, concat_axis=0, tiled=True)
    dots_own, dots_other = halves_of(dots_owned.T, part_index)
    grad_gates = dots_own + swap_tp(dots_other)

    grad_slot = (cotangent_slot * gate_slot[:, :, None]).astype(bf16)
    grad_slot = grad_slot.reshape(slot_count, model_width)
    grad_act = dot(grad_slot, down_mat, ((1,), (1,)))
    grad_gate_pre = (grad_act * up_pre * gate_sig * (1.0 + gate_pre * (1.0 - gate_sig))).astype(
        bf16
    )
    grad_up_pre = (grad_act * gate_pre * gate_sig).astype(bf16)
    grad_in = (
        dot(grad_gate_pre, gate_mat, ((1,), (1,))) + dot(grad_up_pre, up_mat, ((1,), (1,)))
    ).astype(bf16)
    grad_rows = spread(grad_in.reshape(fsdp_count, capacity, model_width)).astype(bf16)
    grad_group = lax.psum_scatter(
        grad_rows.reshape(-1, model_width), "fsdp", scatter_dimension=0, tiled=True
    )
    grad_down = dot(activation, grad_slot, ((0,), (0,)))
    grad_gate = dot(arrived, grad_gate_pre, ((0,), (0,)))
    grad_up = dot(arrived, grad_up_pre, ((0,), (0,)))

    def own_sum(group_rows):
        own, other = halves_of(group_rows, part_index)
        return own.astype(f32) + swap_tp(other).astype(f32)

    own_ids, _ = halves_of(expert_ids, part_index)
    gates_own = gates_of(normed_two, chosen_mask(own_ids))
    grad_logits = (
        gates_own * (grad_gates - jnp.sum(gates_own * grad_gates, axis=1, keepdims=True))
    ).astype(bf16)
    grad_router = dot(normed_two, grad_logits, ((0,), (0,)))
    grad_normed_two = own_sum(grad_group) + dot(grad_logits, router_mat, ((1,), (1,)))
    grad_gain_moe = jnp.sum(grad_normed_two * normal_two, axis=0)
    grad_unit_two = grad_normed_two * moe_gain
    grad_hidden = cotangent.astype(f32) + scale_two * (
        grad_unit_two - normal_two * jnp.mean(grad_unit_two * normal_two, axis=1, keepdims=True)
    )
    grad_attn_own = grad_hidden.astype(bf16)
    grad_attn = joined_rows(grad_attn_own, swap_tp(grad_attn_own), part_index)

    grad_output = dot(grad_attn, context_flat, ((0,), (0,)))
    grad_output = lax.psum_scatter(grad_output.astype(bf16), "fsdp", scatter_dimension=0, tiled=True)
    moe_group = lax.psum_scatter(moe_out, "fsdp", scatter_dimension=0, tiled=True)
    grad_context = (
        dot(grad_attn, out_mat_t, ((1,), (0,))).astype(bf16).reshape(group_len, heads_local, HEAD)
    )
    grad_value_rows = (
        jnp.einsum("hqk,qhd->khd", probs_low, grad_context, preferred_element_type=f32)
        .reshape(group_len, -1)
        .astype(bf16)
    )
    grad_probs = jnp.einsum("qhd,khd->hqk", grad_context, value_heads, preferred_element_type=f32)
    grad_scores = (
        attn_probs * (grad_probs - jnp.sum(attn_probs * grad_probs, axis=-1, keepdims=True))
    ).astype(bf16)
    grad_query_rot = rounded(
        jnp.einsum("hqk,khd->qhd", grad_scores, key_rot, preferred_element_type=f32) * score_scale
    )
    grad_key_rot = rounded(
        jnp.einsum("hqk,qhd->khd", grad_scores, query_rot, preferred_element_type=f32) * score_scale
    )

    def unrotate(grad_heads):
        return (
            grad_heads * cosine_table[:, None, :] + rotate_back(grad_heads * sine_table[:, None, :])
        ).reshape(group_len, -1)

    grad_query_norm = unrotate(grad_query_rot)
    grad_key_norm = unrotate(grad_key_rot)
    sums = jnp.stack(
        [
            jnp.sum(grad_query_norm * query_gain_flat * query_unit, axis=1),
            jnp.sum(grad_key_norm * key_gain_flat * key_unit, axis=1),
        ]
    )
    sums = (sums + swap_tp(sums)) / model_width
    grad_query_raw = (
        query_scale * (query_gain_flat * grad_query_norm - query_unit * sums[0][:, None])
    ).astype(bf16)
    grad_key_raw = (
        key_scale * (key_gain_flat * grad_key_norm - key_unit * sums[1][:, None])
    ).astype(bf16)
    grad_gain_query = jnp.sum(grad_query_norm * query_unit, axis=0)
    grad_gain_key = jnp.sum(grad_key_norm * key_unit, axis=0)
    grad_qkv_raw = jnp.concatenate([grad_query_raw, grad_key_raw, grad_value_rows], axis=1)
    grad_qkv = dot(normed_one, grad_qkv_raw, ((0,), (0,))).astype(bf16)
    grad_qkv = lax.psum_scatter(grad_qkv, "fsdp", scatter_dimension=0, tiled=True)
    grad_normed_part = dot(grad_qkv_raw, qkv_mat, ((1,), (1,))).astype(bf16)
    grad_normed_one = own_sum(grad_normed_part)
    scale_own = rms_scale(tokens_own)
    normal_own = tokens_own * scale_own
    grad_gain_attn = jnp.sum(grad_normed_one * normal_own, axis=0)
    grad_unit_one = grad_normed_one * attn_gain
    grad_tokens = grad_hidden + scale_own * (
        grad_unit_one - normal_own * jnp.mean(grad_unit_one * normal_own, axis=1, keepdims=True)
    )
    block_out = hidden + own_sum(moe_group)

    row_part = jnp.concatenate(
        [
            grad_router.reshape(fsdp_count, -1),
            grad_gain_moe.reshape(fsdp_count, -1),
            grad_gain_attn.reshape(fsdp_count, -1),
        ],
        axis=1,
    )
    row_part = row_part + swap_tp(row_part)

    def by_owner(gain_grad):
        pieces = gain_grad.reshape(heads_local, fsdp_count, gain_cols)
        return jnp.transpose(pieces, (1, 0, 2)).reshape(fsdp_count, -1)

    parcel = jnp.concatenate([row_part, by_owner(grad_gain_query), by_owner(grad_gain_key)], axis=1)
    parcel = lax.all_to_all(parcel, "fsdp", split_axis=0, concat_axis=0, tiled=True)
    parcel = jnp.sum(parcel, axis=0)
    edges = [shard_rows * expert_count, shard_rows, shard_rows, gain_query.size, gain_key.size]
    pieces, start = [], 0
    for size in edges:
        pieces.append(parcel[start : start + size])
        start += size
    grad_qkv = grad_qkv.astype(f32)
    return (
        block_out,
        grad_tokens,
        grad_qkv[:, :half_width],
        grad_qkv[:, half_width : 2 * half_width],
        grad_qkv[:, 2 * half_width :],
        grad_output.astype(f32).T,
        pieces[3].reshape(gain_query.shape),
        pieces[4].reshape(gain_key.shape),
        pieces[2],
        pieces[1],
        pieces[0].reshape(w_router.shape),
        grad_gate[None],
        grad_up[None],
        grad_down[None],
    )


def body(*args):
    topk_count = args[14].shape[1]
    expert_count, local_experts = args[10].shape[1], args[11].shape[0]
    if local_experts == 1 and lax.axis_size("tp") == 2 and expert_count <= 2 * topk_count:
        return dense_body(*args)
    return sparse_body(*args)


def solution(mesh):
    in_specs = (
        P(("fsdp", "tp"), None),
        P(("fsdp", "tp"), None),
        P("fsdp", "tp"),
        P("fsdp", "tp"),
        P("fsdp", "tp"),
        P("tp", "fsdp"),
        P("tp", "fsdp"),
        P("tp", "fsdp"),
        P("fsdp"),
        P("fsdp"),
        P("fsdp", None),
        P("fsdp", None, "tp"),
        P("fsdp", None, "tp"),
        P("fsdp", "tp", None),
        P("fsdp", None),
    )
    out_specs = (
        P(("fsdp", "tp"), None),
        P(("fsdp", "tp"), None),
        P("fsdp", "tp"),
        P("fsdp", "tp"),
        P("fsdp", "tp"),
        P("tp", "fsdp"),
        P("tp", "fsdp"),
        P("tp", "fsdp"),
        P("fsdp"),
        P("fsdp"),
        P("fsdp", None),
        P("fsdp", None, "tp"),
        P("fsdp", None, "tp"),
        P("fsdp", "tp", None),
    )
    return jax.shard_map(body, mesh=mesh, in_specs=in_specs, out_specs=out_specs, check_vma=False)
```

```python
import jax
import jax.numpy as jnp
from jax import lax
from jax.sharding import PartitionSpec as P


HEAD = 128
PROMPT = 128
CONT_LEN = 64


epsilon = 1e-05
theta_base = 10000.0
masked_score = -1e30


def rms_scale(values):
    return lax.rsqrt(jnp.mean(values * values, axis=-1, keepdims=True) + epsilon)


def rotate_half(values):
    middle = values.shape[-1] // 2
    return jnp.concatenate([-values[..., middle:], values[..., :middle]], axis=-1)


def rotate_back(values):
    middle = values.shape[-1] // 2
    return jnp.concatenate([values[..., middle:], -values[..., :middle]], axis=-1)


def positions_of(group_len):
    row_index = jnp.arange(group_len, dtype=jnp.int32)
    return jnp.where(row_index < PROMPT, row_index, PROMPT + (row_index - PROMPT) % CONT_LEN)


def attend_mask(group_len):
    row_index = jnp.arange(group_len, dtype=jnp.int32)
    query_pos = row_index[:, None]
    key_pos = row_index[None, :]
    query_cont = (query_pos - PROMPT) // CONT_LEN
    key_cont = (key_pos - PROMPT) // CONT_LEN
    return (key_pos <= query_pos) & ((key_pos < PROMPT) | (query_cont == key_cont))


def rotary_tables(group_len):
    where_pos = positions_of(group_len).astype(jnp.float32)
    frequency = theta_base ** (-2.0 * jnp.arange(HEAD // 2, dtype=jnp.float32) / HEAD)
    angles = where_pos[:, None] * frequency[None, :]
    angles = jnp.concatenate([angles, angles], axis=1)
    return (jnp.cos(angles), jnp.sin(angles))


def rounded(values):
    return lax.optimization_barrier(values.astype(jnp.bfloat16)).astype(jnp.float32)


def head_sums(first, second):
    return lax.psum((first, second), "tp")


def send_slots(block):
    return lax.all_to_all(block, "fsdp", split_axis=0, concat_axis=0, tiled=True)


def return_slots(block):
    return lax.all_to_all(block, "fsdp", split_axis=0, concat_axis=0, tiled=True)


def sparse_body(
    tokens_in,
    cotangent,
    w_query,
    w_key,
    w_value,
    w_output,
    gain_query,
    gain_key,
    gain_attn,
    gain_moe,
    w_router,
    w_gate,
    w_up,
    w_down,
    expert_ids,
):
    fsdp_count = lax.axis_size("fsdp")
    part_index = lax.axis_index("tp")
    own_rows = tokens_in.shape[0]
    start_row = part_index * own_rows

    def gather_params():
        return (
            lax.all_gather(w_query, "fsdp", axis=0, tiled=True),
            lax.all_gather(w_key, "fsdp", axis=0, tiled=True),
            lax.all_gather(w_value, "fsdp", axis=0, tiled=True),
            lax.all_gather(w_output, "fsdp", axis=1, tiled=True),
            lax.all_gather(gain_query, "fsdp", axis=1, tiled=True),
            lax.all_gather(gain_key, "fsdp", axis=1, tiled=True),
            lax.all_gather(gain_attn, "fsdp", axis=0, tiled=True),
            lax.all_gather(gain_moe, "fsdp", axis=0, tiled=True),
            lax.all_gather(w_router, "fsdp", axis=0, tiled=True),
        )

    (
        query_mat,
        key_mat,
        value_mat,
        output_mat,
        query_gain,
        key_gain,
        attn_gain,
        moe_gain,
        router_mat,
    ) = gather_params()
    rows_all, grad_rows = (
        lax.all_gather(tokens_in, "tp", axis=0, tiled=True),
        lax.all_gather(cotangent, "tp", axis=0, tiled=True),
    )
    group_len = rows_all.shape[0]
    model_width = rows_all.shape[1]
    topk_count = expert_ids.shape[1]
    expert_count = router_mat.shape[1]
    local_experts = w_gate.shape[0]
    capacity = (group_len * topk_count * 7 // (6 * expert_count) + 7) // 8 * 8
    slot_count = expert_count * capacity
    residual_in = rows_all.astype(jnp.float32)
    scale_one = rms_scale(residual_in)
    normal_one = residual_in * scale_one
    normed_one = (normal_one * attn_gain.astype(jnp.float32)).astype(jnp.bfloat16)
    query_raw = jnp.dot(normed_one, query_mat, preferred_element_type=jnp.float32)
    key_raw = jnp.dot(normed_one, key_mat, preferred_element_type=jnp.float32)
    value_flat = jnp.dot(normed_one, value_mat, preferred_element_type=jnp.float32).astype(
        jnp.bfloat16
    )
    query_sq, key_sq = head_sums(
        jnp.sum(query_raw * query_raw, axis=1), jnp.sum(key_raw * key_raw, axis=1)
    )
    query_scale = lax.rsqrt(query_sq / model_width + epsilon)[:, None]
    key_scale = lax.rsqrt(key_sq / model_width + epsilon)[:, None]
    heads_local = query_gain.shape[0]
    query_gain_flat = query_gain.astype(jnp.float32).reshape(-1)
    key_gain_flat = key_gain.astype(jnp.float32).reshape(-1)
    query_unit = query_raw * query_scale
    key_unit = key_raw * key_scale
    cosine_table, sine_table = rotary_tables(group_len)

    def rotate(matrix):
        pieces = matrix.reshape(group_len, heads_local, HEAD)
        return pieces * cosine_table[:, None, :] + rotate_half(pieces) * sine_table[:, None, :]

    query_rot = rotate(query_unit * query_gain_flat).astype(jnp.bfloat16)
    key_rot = rotate(key_unit * key_gain_flat).astype(jnp.bfloat16)
    value_heads = value_flat.reshape(group_len, heads_local, HEAD)
    allowed = attend_mask(group_len)[None]
    score_scale = HEAD ** (-0.5)

    def scores_now():
        raw_scores = (
            jnp.einsum("qhd,khd->hqk", query_rot, key_rot, preferred_element_type=jnp.float32)
            * score_scale
        )
        return jnp.where(allowed, raw_scores, masked_score)

    scores = scores_now()
    row_top = jnp.max(scores, axis=-1, keepdims=True)
    exp_scores = jnp.exp(scores - row_top)
    exp_total = jnp.sum(exp_scores, axis=-1, keepdims=True)
    log_total = row_top + jnp.log(exp_total)
    context = jnp.einsum(
        "hqk,khd->qhd",
        (exp_scores / exp_total).astype(jnp.bfloat16),
        value_heads,
        preferred_element_type=jnp.float32,
    )
    context_flat = context.reshape(group_len, -1).astype(jnp.bfloat16)
    attn_out = lax.psum(jnp.dot(context_flat, output_mat, preferred_element_type=jnp.float32), "tp")
    hidden = residual_in + attn_out
    scale_two = rms_scale(hidden)
    normal_two = hidden * scale_two
    normed_two = (normal_two * moe_gain.astype(jnp.float32)).astype(jnp.bfloat16)
    logits = jnp.dot(normed_two, router_mat, preferred_element_type=jnp.float32)
    onehot = expert_ids[:, :, None] == jnp.arange(expert_count, dtype=jnp.int32)[None, None, :]
    chosen = jnp.sum(jnp.where(onehot, logits[:, None, :], 0.0), axis=2)
    gate_probs = jax.nn.softmax(chosen, axis=-1)
    per_token = jnp.sum(onehot.astype(jnp.float32), axis=1)
    row_index = jnp.arange(group_len, dtype=jnp.int32)
    earlier = (row_index[None, :] < row_index[:, None]).astype(jnp.float32)
    before = jnp.dot(earlier, per_token, preferred_element_type=jnp.float32)
    slot_index = jnp.sum(jnp.where(onehot, before[:, None, :], 0.0), axis=2).astype(jnp.int32)
    slot_dest = expert_ids * capacity + slot_index
    flat_dest = slot_dest.reshape(-1)
    token_of_slot = (
        jnp.full((slot_count,), group_len, jnp.int32)
        .at[flat_dest]
        .set(jnp.repeat(row_index, topk_count))
    )
    gate_of_slot = jnp.zeros((slot_count,), jnp.float32).at[flat_dest].set(gate_probs.reshape(-1))
    slot_mine = slot_index >= 0
    normed_pad = jnp.concatenate([normed_two, jnp.zeros((1, model_width), jnp.bfloat16)], axis=0)
    cotangent_pad = jnp.concatenate([grad_rows, jnp.zeros((1, model_width), jnp.bfloat16)], axis=0)
    send_shape = (fsdp_count, local_experts, capacity, model_width)
    outgoing = normed_pad[token_of_slot].reshape(send_shape)
    arrived = send_slots(outgoing)
    gate_pre = jnp.einsum("secd,edf->secf", arrived, w_gate, preferred_element_type=jnp.float32)
    up_pre = jnp.einsum("secd,edf->secf", arrived, w_up, preferred_element_type=jnp.float32)
    gate_pre, up_pre, activation = (
        gate_pre,
        up_pre,
        (jax.nn.silu(gate_pre) * up_pre).astype(jnp.bfloat16),
    )
    partial_value = jnp.einsum(
        "secf,efd->secd", activation, w_down, preferred_element_type=jnp.float32
    ).astype(jnp.bfloat16)
    returned = return_slots(partial_value).reshape(-1, model_width)
    cotangent_full = grad_rows.astype(jnp.float32)
    moe_part = jnp.zeros((group_len, model_width), jnp.float32)
    gate_terms = []
    for column in range(topk_count):
        picked = jnp.where(
            slot_mine[:, column : column + 1],
            returned[slot_dest[:, column]].astype(jnp.float32),
            0.0,
        )
        moe_part = moe_part + gate_probs[:, column : column + 1] * picked
        gate_terms.append(jnp.sum(cotangent_full * picked, axis=1))
    moe_own = lax.psum_scatter(
        moe_part.astype(jnp.bfloat16), "tp", scatter_dimension=0, tiled=True
    ).astype(jnp.float32)
    block_out = lax.dynamic_slice_in_dim(hidden, start_row, own_rows, 0) + moe_own
    (
        query_mat,
        key_mat,
        value_mat,
        output_mat,
        query_gain,
        key_gain,
        attn_gain,
        moe_gain,
        router_mat,
    ) = gather_params()
    grad_slot = (
        (cotangent_pad[token_of_slot].astype(jnp.float32) * gate_of_slot[:, None])
        .astype(jnp.bfloat16)
        .reshape(send_shape)
    )
    grad_partial = send_slots(grad_slot)
    grad_act = jnp.einsum(
        "secd,efd->secf", grad_partial, w_down, preferred_element_type=jnp.float32
    )
    grad_down = jnp.einsum(
        "secf,secd->efd", activation, grad_partial, preferred_element_type=jnp.float32
    )
    gate_sig = jax.nn.sigmoid(gate_pre)
    grad_gate_pre = (grad_act * up_pre * gate_sig * (1.0 + gate_pre * (1.0 - gate_sig))).astype(
        jnp.bfloat16
    )
    grad_up_pre = (grad_act * gate_pre * gate_sig).astype(jnp.bfloat16)
    grad_gate = jnp.einsum(
        "secd,secf->edf", arrived, grad_gate_pre, preferred_element_type=jnp.float32
    )
    grad_up = jnp.einsum("secd,secf->edf", arrived, grad_up_pre, preferred_element_type=jnp.float32)
    grad_in = (
        jnp.einsum("secf,edf->secd", grad_gate_pre, w_gate, preferred_element_type=jnp.float32)
        + jnp.einsum("secf,edf->secd", grad_up_pre, w_up, preferred_element_type=jnp.float32)
    ).astype(jnp.bfloat16)
    grad_back = return_slots(grad_in).reshape(-1, model_width)
    grad_normed_part = jnp.zeros((group_len, model_width), jnp.float32)
    for column in range(topk_count):
        grad_normed_part = grad_normed_part + jnp.where(
            slot_mine[:, column : column + 1],
            grad_back[slot_dest[:, column]].astype(jnp.float32),
            0.0,
        )
    grad_normed_moe, grad_gate_probs = lax.psum(
        (grad_normed_part, jnp.stack(gate_terms, axis=1)), "tp"
    )
    grad_chosen = gate_probs * (
        grad_gate_probs - jnp.sum(gate_probs * grad_gate_probs, axis=1, keepdims=True)
    )
    grad_logits = jnp.sum(jnp.where(onehot, grad_chosen[:, :, None], 0.0), axis=1).astype(
        jnp.bfloat16
    )
    grad_router = jnp.einsum(
        "td,te->de", normed_two, grad_logits, preferred_element_type=jnp.float32
    )
    grad_normed_two = grad_normed_moe + jnp.einsum(
        "te,de->td", grad_logits, router_mat, preferred_element_type=jnp.float32
    )
    grad_gain_moe = jnp.sum(grad_normed_two * normal_two, axis=0)
    grad_unit_two = grad_normed_two * moe_gain.astype(jnp.float32)
    grad_hidden = cotangent_full + scale_two * (
        grad_unit_two - normal_two * jnp.mean(grad_unit_two * normal_two, axis=1, keepdims=True)
    )
    grad_attn = grad_hidden.astype(jnp.bfloat16)
    grad_output = jnp.einsum(
        "tc,td->cd", context_flat, grad_attn, preferred_element_type=jnp.float32
    )
    grad_context = (
        jnp.einsum("td,cd->tc", grad_attn, output_mat, preferred_element_type=jnp.float32)
        .astype(jnp.bfloat16)
        .reshape(group_len, heads_local, HEAD)
    )
    attn_probs = jnp.exp(scores_now() - log_total)
    grad_value_rows = (
        jnp.einsum(
            "hqk,qhd->khd",
            attn_probs.astype(jnp.bfloat16),
            grad_context,
            preferred_element_type=jnp.float32,
        )
        .reshape(group_len, -1)
        .astype(jnp.bfloat16)
    )
    grad_probs = jnp.einsum(
        "qhd,khd->hqk", grad_context, value_heads, preferred_element_type=jnp.float32
    )
    grad_scores = (
        attn_probs * (grad_probs - jnp.sum(attn_probs * grad_probs, axis=-1, keepdims=True))
    ).astype(jnp.bfloat16)
    grad_query_rot = rounded(
        jnp.einsum("hqk,khd->qhd", grad_scores, key_rot, preferred_element_type=jnp.float32)
        * score_scale
    )
    grad_key_rot = rounded(
        jnp.einsum("hqk,qhd->khd", grad_scores, query_rot, preferred_element_type=jnp.float32)
        * score_scale
    )

    def unrotate(grad_heads):
        return (
            grad_heads * cosine_table[:, None, :] + rotate_back(grad_heads * sine_table[:, None, :])
        ).reshape(group_len, -1)

    grad_query_norm = unrotate(grad_query_rot)
    grad_key_norm = unrotate(grad_key_rot)
    sum_query, sum_key = head_sums(
        jnp.sum(grad_query_norm * query_gain_flat * query_unit, axis=1),
        jnp.sum(grad_key_norm * key_gain_flat * key_unit, axis=1),
    )
    grad_query_raw = (
        query_scale
        * (query_gain_flat * grad_query_norm - query_unit * (sum_query / model_width)[:, None])
    ).astype(jnp.bfloat16)
    grad_key_raw = (
        key_scale * (key_gain_flat * grad_key_norm - key_unit * (sum_key / model_width)[:, None])
    ).astype(jnp.bfloat16)
    grad_gain_query = jnp.sum(grad_query_norm * query_unit, axis=0).reshape(heads_local, HEAD)
    grad_gain_key = jnp.sum(grad_key_norm * key_unit, axis=0).reshape(heads_local, HEAD)
    grad_query = jnp.einsum(
        "td,tc->dc", normed_one, grad_query_raw, preferred_element_type=jnp.float32
    )
    grad_key = jnp.einsum("td,tc->dc", normed_one, grad_key_raw, preferred_element_type=jnp.float32)
    grad_value = jnp.einsum(
        "td,tc->dc", normed_one, grad_value_rows, preferred_element_type=jnp.float32
    )
    grad_normed_local = (
        jnp.einsum("tc,dc->td", grad_query_raw, query_mat, preferred_element_type=jnp.float32)
        + jnp.einsum("tc,dc->td", grad_key_raw, key_mat, preferred_element_type=jnp.float32)
        + jnp.einsum("tc,dc->td", grad_value_rows, value_mat, preferred_element_type=jnp.float32)
    )
    grad_normed_one = lax.psum(grad_normed_local.astype(jnp.bfloat16), "tp").astype(jnp.float32)
    grad_gain_attn = jnp.sum(grad_normed_one * normal_one, axis=0)
    grad_unit_one = grad_normed_one * attn_gain.astype(jnp.float32)
    grad_full = grad_hidden + scale_one * (
        grad_unit_one - normal_one * jnp.mean(grad_unit_one * normal_one, axis=1, keepdims=True)
    )
    grad_tokens = lax.dynamic_slice_in_dim(grad_full, start_row, own_rows, 0)
    sharded = (
        lax.psum_scatter(grad_query, "fsdp", scatter_dimension=0, tiled=True),
        lax.psum_scatter(grad_key, "fsdp", scatter_dimension=0, tiled=True),
        lax.psum_scatter(grad_value, "fsdp", scatter_dimension=0, tiled=True),
        lax.psum_scatter(grad_output, "fsdp", scatter_dimension=1, tiled=True),
        lax.psum_scatter(grad_gain_query, "fsdp", scatter_dimension=1, tiled=True),
        lax.psum_scatter(grad_gain_key, "fsdp", scatter_dimension=1, tiled=True),
        lax.psum_scatter(grad_gain_attn, "fsdp", scatter_dimension=0, tiled=True),
        lax.psum_scatter(grad_gain_moe, "fsdp", scatter_dimension=0, tiled=True),
        lax.psum_scatter(grad_router, "fsdp", scatter_dimension=0, tiled=True),
    )
    return (
        block_out,
        grad_tokens,
        sharded[0],
        sharded[1],
        sharded[2],
        sharded[3],
        sharded[4],
        sharded[5],
        sharded[6],
        sharded[7],
        sharded[8],
        grad_gate,
        grad_up,
        grad_down,
    )


def swap_tp(values):
    return lax.ppermute(values, "tp", [(0, 1), (1, 0)])


def joined_rows(own, other, part_index):
    first = jnp.where(part_index == 0, own, other)
    second = jnp.where(part_index == 0, other, own)
    return jnp.concatenate([first, second], axis=0)


def halves_of(values, part_index):
    rows = values.shape[0] // 2
    low, high = values[:rows], values[rows:]
    return jnp.where(part_index == 0, low, high), jnp.where(part_index == 0, high, low)


def fsdp_swap(values, stride, fsdp_count):
    return lax.ppermute(values, "fsdp", [(i, i ^ stride) for i in range(fsdp_count)])


def line_shift(values, senders, step, fsdp_count):
    planes = fsdp_count // 4
    pairs = [(z * 4 + low, (z + step) * 4 + low) for z in senders for low in range(4)]
    return lax.ppermute(values, "fsdp", [p for p in pairs if 0 <= p[1] < planes * 4])


def line_gather(own, plane, fsdp_count):
    planes = fsdp_count // 4
    right, left, from_low, from_high = own, own, [], []
    for step in range(1, planes):
        right = line_shift(right, range(step - 1, planes - 1), 1, fsdp_count)
        left = line_shift(left, range(1, planes - step + 1), -1, fsdp_count)
        from_low.append(right)
        from_high.append(left)
    relative = [own]
    for step in range(1, planes):
        relative.append(jnp.where(plane >= step, from_low[step - 1], from_high[planes - step - 1]))
    wheel = [relative[(planes - 1 - i) % planes] for i in range(2 * planes - 1)]
    return lax.dynamic_slice_in_dim(jnp.stack(wheel), planes - 1 - plane, planes, 0)


def line_scatter(parts, plane, fsdp_count):
    planes = fsdp_count // 4
    wide = jnp.float32

    def part(index):
        return lax.dynamic_index_in_dim(parts, jnp.clip(index, 0, planes - 1), 0, keepdims=False)

    right, left = None, None
    for step in range(1, planes):
        send_right = part(plane + planes - step)
        send_left = part(plane - planes + step)
        if step > 1:
            send_right = (send_right.astype(wide) + right.astype(wide)).astype(parts.dtype)
            send_left = (send_left.astype(wide) + left.astype(wide)).astype(parts.dtype)
        right = line_shift(send_right, range(0, min(step, planes - 1)), 1, fsdp_count)
        left = line_shift(send_left, range(max(planes - step, 1), planes), -1, fsdp_count)
    total = part(plane).astype(wide)
    if planes > 1:
        total = total + right.astype(wide) + left.astype(wide)
    return total


def ordered(own, other, index, axis):
    return jnp.stack([jnp.where(index == 0, own, other), jnp.where(index == 0, other, own)], axis)


def dense_body(
    tokens_in,
    cotangent,
    w_query,
    w_key,
    w_value,
    w_output,
    gain_query,
    gain_key,
    gain_attn,
    gain_moe,
    w_router,
    w_gate,
    w_up,
    w_down,
    expert_ids,
):
    f32, bf16 = jnp.float32, jnp.bfloat16
    fsdp_count = lax.axis_size("fsdp")
    part_index = lax.axis_index("tp")
    expert_index = lax.axis_index("fsdp")
    own_rows, model_width = tokens_in.shape
    group_len = 2 * own_rows
    half_width = w_query.shape[1]
    topk_count = expert_ids.shape[1]
    expert_count = w_router.shape[1]
    shard_rows = w_query.shape[0]
    heads_local = gain_query.shape[0]
    gain_cols = gain_query.shape[1]
    capacity = (group_len * topk_count * 7 // (6 * expert_count) + 7) // 8 * 8

    def dot(left, right, dims):
        return lax.dot_general(left, right, (dims, ((), ())), preferred_element_type=f32)

    def column(flat):
        return jnp.pad(flat, (0, shard_rows - flat.shape[0]))[:, None]

    expert_row = jnp.arange(expert_count, dtype=jnp.int32)
    mask_group = jnp.any(expert_ids[:, :, None] == expert_row[None, None, :], axis=1)
    mask_packed = mask_group.astype(bf16).reshape(shard_rows, -1)
    mask_cols = mask_packed.shape[1]
    small = jnp.concatenate(
        [
            w_router,
            gain_attn[:, None],
            gain_moe[:, None],
            column(gain_query.reshape(-1)),
            column(gain_key.reshape(-1)),
            mask_packed,
        ],
        axis=1,
    )
    small_cols = small.shape[1]
    small = jnp.pad(small, ((0, 0), (0, -small_cols % 128)))
    packed = jnp.concatenate([w_query, w_key, w_value, small], axis=1)
    packed_all = lax.all_gather(packed, "fsdp", axis=0, tiled=True)
    plane, row_y, core = expert_index // 4, expert_index // 2 % 2, expert_index % 2
    planes = fsdp_count // 4
    cot_line = line_gather(cotangent, plane, fsdp_count)
    cot_line = ordered(cot_line, fsdp_swap(cot_line, 2, fsdp_count), row_y, 1)
    packed_all, cot_line = lax.optimization_barrier((packed_all, cot_line))
    cot_across = swap_tp(cot_line)
    cot_core = ordered(cot_line, cot_across, part_index, 2)
    cot_core = cot_core.reshape(2 * planes, group_len, model_width)
    cot_partner = fsdp_swap(cot_core, 1, fsdp_count)

    qkv_mat = packed_all[:, : 3 * half_width]
    small_all = packed_all[:, 3 * half_width :]
    router_mat = small_all[:, :expert_count]
    attn_gain = small_all[:, expert_count].astype(f32)
    moe_gain = small_all[:, expert_count + 1].astype(f32)

    def head_gain(index):
        flat = small_all[:, expert_count + 2 + index].reshape(fsdp_count, shard_rows)
        flat = flat[:, : heads_local * gain_cols].reshape(fsdp_count, heads_local, gain_cols)
        return jnp.transpose(flat, (1, 0, 2)).reshape(-1).astype(f32)

    query_gain_flat, key_gain_flat = head_gain(0), head_gain(1)
    out_mat_t = lax.all_gather(w_output.T, "fsdp", axis=0, tiled=True)
    mask_all = small_all[:, small_cols - mask_cols : small_cols].reshape(-1, expert_count) > 0

    residual_in = joined_rows(tokens_in, swap_tp(tokens_in), part_index).astype(f32)
    scale_one = rms_scale(residual_in)
    normed_one = (residual_in * scale_one * attn_gain).astype(bf16)
    qkv = dot(normed_one, qkv_mat, ((1,), (0,)))
    query_raw = qkv[:, :half_width]
    key_raw = qkv[:, half_width : 2 * half_width]
    value_flat = qkv[:, 2 * half_width :].astype(bf16)
    squares = jnp.stack(
        [jnp.sum(query_raw * query_raw, axis=1), jnp.sum(key_raw * key_raw, axis=1)]
    )
    squares = squares + swap_tp(squares)
    query_scale = lax.rsqrt(squares[0] / model_width + epsilon)[:, None]
    key_scale = lax.rsqrt(squares[1] / model_width + epsilon)[:, None]
    query_unit = query_raw * query_scale
    key_unit = key_raw * key_scale
    cosine_table, sine_table = rotary_tables(group_len)

    def rotate(matrix):
        pieces = matrix.reshape(group_len, heads_local, HEAD)
        return pieces * cosine_table[:, None, :] + rotate_half(pieces) * sine_table[:, None, :]

    query_rot = rotate(query_unit * query_gain_flat).astype(bf16)
    key_rot = rotate(key_unit * key_gain_flat).astype(bf16)
    value_heads = value_flat.reshape(group_len, heads_local, HEAD)
    allowed = attend_mask(group_len)[None]
    score_scale = HEAD ** (-0.5)
    raw_scores = (
        jnp.einsum("qhd,khd->hqk", query_rot, key_rot, preferred_element_type=f32) * score_scale
    )
    scores = jnp.where(allowed, raw_scores, masked_score)
    row_top = jnp.max(scores, axis=-1, keepdims=True)
    exp_scores = jnp.exp(scores - row_top)
    attn_probs = exp_scores / jnp.sum(exp_scores, axis=-1, keepdims=True)
    probs_low = attn_probs.astype(bf16)
    context = jnp.einsum("hqk,khd->qhd", probs_low, value_heads, preferred_element_type=f32)
    context_flat = context.reshape(group_len, -1).astype(bf16)
    attn_part = dot(context_flat, out_mat_t, ((1,), (1,)))
    attn_own, attn_other = halves_of(attn_part, part_index)
    tokens_own = tokens_in.astype(f32)
    hidden = tokens_own + (attn_own + swap_tp(attn_other.astype(bf16)).astype(f32))
    scale_two = rms_scale(hidden)
    normal_two = hidden * scale_two
    normed_two = (normal_two * moe_gain).astype(bf16)

    both = ("fsdp", "tp")
    rows_all = lax.all_gather(normed_two, both, axis=0, tiled=True)

    def gates_of(rows, mask):
        logits = jnp.where(mask, dot(rows, router_mat, ((1,), (0,))), -jnp.inf)
        top = jnp.max(logits, axis=1, keepdims=True)
        weights = jnp.where(mask, jnp.exp(logits - top), 0.0)
        return weights / jnp.sum(weights, axis=1, keepdims=True)

    gates_all = gates_of(rows_all, mask_all)
    gate_here = jnp.sum(jnp.where(expert_row[None, :] == expert_index, gates_all, 0.0), axis=1)
    gate_here = gate_here.reshape(fsdp_count, group_len)
    named = jnp.any(mask_all & (expert_row[None, :] == expert_index), axis=1)
    named = named.reshape(fsdp_count, group_len)
    row_index = jnp.arange(group_len, dtype=jnp.int32)
    earlier = (row_index[:, None] < row_index[None, :]).astype(bf16)
    place = dot(named.astype(bf16), earlier, ((1,), (0,))).astype(jnp.int32)
    slot_row = jnp.arange(capacity, dtype=jnp.int32)
    select = (slot_row[None, :, None] == place[:, None, :]) & named[:, None, :]
    select_low = select.astype(bf16)
    gate_slot = jnp.sum(jnp.where(select, gate_here[:, None, :], 0.0), axis=2)

    def pick(chosen, rows):
        return jnp.einsum("gct,gtd->gcd", chosen, rows, preferred_element_type=f32).astype(bf16)

    def spread(chosen, slots):
        return jnp.einsum("gct,gcd->gtd", chosen, slots, preferred_element_type=f32)

    def of_core(values, index):
        paired = values.reshape((2 * planes, 2) + values.shape[1:])
        return lax.dynamic_index_in_dim(paired, index, 1, keepdims=False)

    select_mine, select_partner = of_core(select_low, core), of_core(select_low, 1 - core)

    slot_count = fsdp_count * capacity
    arrived = pick(select_low, rows_all.reshape(fsdp_count, group_len, model_width))
    arrived = arrived.reshape(slot_count, model_width)
    gate_mat, up_mat, down_mat = w_gate[0], w_up[0], w_down[0]
    gate_pre = dot(arrived, gate_mat, ((1,), (0,)))
    up_pre = dot(arrived, up_mat, ((1,), (0,)))
    gate_sig = jax.nn.sigmoid(gate_pre)
    activation = (gate_pre * gate_sig * up_pre).astype(bf16)
    partial_value = dot(activation, down_mat, ((1,), (0,))).astype(bf16)
    partial_value = partial_value.reshape(fsdp_count, capacity, model_width)
    cotangent_slot = ordered(
        pick(select_mine, cot_core), pick(select_partner, cot_partner), core, 1
    )
    cotangent_slot = cotangent_slot.reshape(fsdp_count, capacity, model_width).astype(f32)
    slot_dots = jnp.sum(cotangent_slot * partial_value.astype(f32), axis=2)
    token_dots = jnp.sum(jnp.where(select, slot_dots[:, :, None], 0.0), axis=1)

    dots_owned = lax.all_to_all(token_dots, "fsdp", split_axis=0, concat_axis=0, tiled=True)
    dots_own, dots_other = halves_of(dots_owned.T, part_index)
    grad_gates = dots_own + swap_tp(dots_other)

    grad_slot = (cotangent_slot * gate_slot[:, :, None]).astype(bf16)
    grad_slot = grad_slot.reshape(slot_count, model_width)
    grad_act = dot(grad_slot, down_mat, ((1,), (1,)))
    grad_gate_pre = (grad_act * up_pre * gate_sig * (1.0 + gate_pre * (1.0 - gate_sig))).astype(
        bf16
    )
    grad_up_pre = (grad_act * gate_pre * gate_sig).astype(bf16)
    grad_in = (
        dot(grad_gate_pre, gate_mat, ((1,), (1,))) + dot(grad_up_pre, up_mat, ((1,), (1,)))
    ).astype(bf16)
    grad_rows = spread(select_low, grad_in.reshape(fsdp_count, capacity, model_width)).astype(bf16)
    grad_rows, partial_value = lax.optimization_barrier((grad_rows, partial_value))

    def weighted(index, chosen):
        slots = of_core(partial_value, index)
        return spread(chosen, slots) * of_core(gate_here, index)[:, :, None]

    moe_away = weighted(1 - core, select_partner).astype(bf16)
    moe_sum = (
        weighted(core, select_mine) + fsdp_swap(moe_away, 1, fsdp_count).astype(f32)
    ).astype(bf16)
    moe_sum = moe_sum.reshape(2 * planes, 2, own_rows, model_width)

    grad_group = lax.psum_scatter(
        grad_rows.reshape(-1, model_width), "fsdp", scatter_dimension=0, tiled=True
    )
    grad_group, moe_sum = lax.optimization_barrier((grad_group, moe_sum))

    def keep_and_send(values, index, axis):
        keep = lax.dynamic_index_in_dim(values, index, axis, keepdims=False)
        return keep, lax.dynamic_index_in_dim(values, 1 - index, axis, keepdims=False)

    moe_keep, moe_away = keep_and_send(moe_sum, part_index, 1)
    moe_across = swap_tp(moe_away)
    moe_sum = (moe_keep.astype(f32) + moe_across.astype(f32)).astype(bf16)
    moe_sum = moe_sum.reshape(planes, 2, own_rows, model_width)
    moe_keep, moe_away = keep_and_send(moe_sum, row_y, 1)
    moe_sum = moe_keep.astype(f32) + fsdp_swap(moe_away, 2, fsdp_count).astype(f32)
    moe_own = line_scatter(moe_sum.astype(bf16), plane, fsdp_count)
    grad_down = dot(activation, grad_slot, ((0,), (0,)))
    grad_gate = dot(arrived, grad_gate_pre, ((0,), (0,)))
    grad_up = dot(arrived, grad_up_pre, ((0,), (0,)))

    def own_sum(group_rows):
        own, other = halves_of(group_rows, part_index)
        return own.astype(f32) + swap_tp(other).astype(f32)

    own_mask, _ = halves_of(mask_group, part_index)
    gates_own = gates_of(normed_two, own_mask)
    grad_logits = (
        gates_own * (grad_gates - jnp.sum(gates_own * grad_gates, axis=1, keepdims=True))
    ).astype(bf16)
    grad_router = dot(normed_two, grad_logits, ((0,), (0,)))
    grad_normed_two = own_sum(grad_group) + dot(grad_logits, router_mat, ((1,), (1,)))
    grad_gain_moe = jnp.sum(grad_normed_two * normal_two, axis=0)
    grad_unit_two = grad_normed_two * moe_gain
    grad_hidden = cotangent.astype(f32) + scale_two * (
        grad_unit_two - normal_two * jnp.mean(grad_unit_two * normal_two, axis=1, keepdims=True)
    )
    grad_attn_own = grad_hidden.astype(bf16)
    grad_attn = joined_rows(grad_attn_own, swap_tp(grad_attn_own), part_index)

    grad_output = dot(grad_attn, context_flat, ((0,), (0,)))
    grad_output = lax.psum_scatter(grad_output.astype(bf16), "fsdp", scatter_dimension=0, tiled=True)
    grad_context = dot(grad_attn, out_mat_t, ((1,), (0,))).astype(bf16)
    grad_context = grad_context.reshape(group_len, heads_local, HEAD)
    grad_value_rows = (
        jnp.einsum("hqk,qhd->khd", probs_low, grad_context, preferred_element_type=f32)
        .reshape(group_len, -1)
        .astype(bf16)
    )
    grad_probs = jnp.einsum("qhd,khd->hqk", grad_context, value_heads, preferred_element_type=f32)
    grad_scores = (
        attn_probs * (grad_probs - jnp.sum(attn_probs * grad_probs, axis=-1, keepdims=True))
    ).astype(bf16)
    grad_query_rot = rounded(
        jnp.einsum("hqk,khd->qhd", grad_scores, key_rot, preferred_element_type=f32) * score_scale
    )
    grad_key_rot = rounded(
        jnp.einsum("hqk,qhd->khd", grad_scores, query_rot, preferred_element_type=f32) * score_scale
    )

    def unrotate(grad_heads):
        return (
            grad_heads * cosine_table[:, None, :] + rotate_back(grad_heads * sine_table[:, None, :])
        ).reshape(group_len, -1)

    grad_query_norm = unrotate(grad_query_rot)
    grad_key_norm = unrotate(grad_key_rot)
    sums = jnp.stack(
        [
            jnp.sum(grad_query_norm * query_gain_flat * query_unit, axis=1),
            jnp.sum(grad_key_norm * key_gain_flat * key_unit, axis=1),
        ]
    )
    sums = (sums + swap_tp(sums)) / model_width
    grad_query_raw = (
        query_scale * (query_gain_flat * grad_query_norm - query_unit * sums[0][:, None])
    ).astype(bf16)
    grad_key_raw = (
        key_scale * (key_gain_flat * grad_key_norm - key_unit * sums[1][:, None])
    ).astype(bf16)
    grad_gain_query = jnp.sum(grad_query_norm * query_unit, axis=0)
    grad_gain_key = jnp.sum(grad_key_norm * key_unit, axis=0)
    grad_qkv_raw = jnp.concatenate([grad_query_raw, grad_key_raw, grad_value_rows], axis=1)
    grad_qkv = dot(normed_one, grad_qkv_raw, ((0,), (0,))).astype(bf16)
    grad_qkv = lax.psum_scatter(grad_qkv, "fsdp", scatter_dimension=0, tiled=True)
    grad_normed_part = dot(grad_qkv_raw, qkv_mat, ((1,), (1,))).astype(bf16)
    grad_normed_one = own_sum(grad_normed_part)
    scale_own = rms_scale(tokens_own)
    normal_own = tokens_own * scale_own
    grad_gain_attn = jnp.sum(grad_normed_one * normal_own, axis=0)
    grad_unit_one = grad_normed_one * attn_gain
    grad_tokens = grad_hidden + scale_own * (
        grad_unit_one - normal_own * jnp.mean(grad_unit_one * normal_own, axis=1, keepdims=True)
    )
    block_out = hidden + moe_own

    row_part = jnp.concatenate(
        [
            grad_router.reshape(fsdp_count, -1),
            grad_gain_moe.reshape(fsdp_count, -1),
            grad_gain_attn.reshape(fsdp_count, -1),
        ],
        axis=1,
    )
    row_part = row_part + swap_tp(row_part)

    def by_owner(gain_grad):
        pieces = gain_grad.reshape(heads_local, fsdp_count, gain_cols)
        return jnp.transpose(pieces, (1, 0, 2)).reshape(fsdp_count, -1)

    parcel = jnp.concatenate([row_part, by_owner(grad_gain_query), by_owner(grad_gain_key)], axis=1)
    parcel = lax.all_to_all(parcel, "fsdp", split_axis=0, concat_axis=0, tiled=True)
    parcel = jnp.sum(parcel, axis=0)
    edges = [shard_rows * expert_count, shard_rows, shard_rows, gain_query.size, gain_key.size]
    pieces, start = [], 0
    for size in edges:
        pieces.append(parcel[start : start + size])
        start += size
    grad_qkv = grad_qkv.astype(f32)
    return (
        block_out,
        grad_tokens,
        grad_qkv[:, :half_width],
        grad_qkv[:, half_width : 2 * half_width],
        grad_qkv[:, 2 * half_width :],
        grad_output.astype(f32).T,
        pieces[3].reshape(gain_query.shape),
        pieces[4].reshape(gain_key.shape),
        pieces[2],
        pieces[1],
        pieces[0].reshape(w_router.shape),
        grad_gate[None],
        grad_up[None],
        grad_down[None],
    )


def body(*args):
    topk_count = args[14].shape[1]
    expert_count, local_experts = args[10].shape[1], args[11].shape[0]
    paired = lax.axis_size("tp") == 2 and lax.axis_size("fsdp") % 4 == 0
    if local_experts == 1 and paired and expert_count <= 2 * topk_count:
        return dense_body(*args)
    return sparse_body(*args)


def solution(mesh):
    in_specs = (
        P(("fsdp", "tp"), None),
        P(("fsdp", "tp"), None),
        P("fsdp", "tp"),
        P("fsdp", "tp"),
        P("fsdp", "tp"),
        P("tp", "fsdp"),
        P("tp", "fsdp"),
        P("tp", "fsdp"),
        P("fsdp"),
        P("fsdp"),
        P("fsdp", None),
        P("fsdp", None, "tp"),
        P("fsdp", None, "tp"),
        P("fsdp", "tp", None),
        P("fsdp", None),
    )
    out_specs = (
        P(("fsdp", "tp"), None),
        P(("fsdp", "tp"), None),
        P("fsdp", "tp"),
        P("fsdp", "tp"),
        P("fsdp", "tp"),
        P("tp", "fsdp"),
        P("tp", "fsdp"),
        P("tp", "fsdp"),
        P("fsdp"),
        P("fsdp"),
        P("fsdp", None),
        P("fsdp", None, "tp"),
        P("fsdp", None, "tp"),
        P("fsdp", "tp", None),
    )
    return jax.shard_map(body, mesh=mesh, in_specs=in_specs, out_specs=out_specs, check_vma=False)
```
